32 devices in a mesh: slab: 4 (over z), xsec: 8 (over y, x, core).
Axes of the slice: x: 2, y: 2, z: 4, core: 2. Of those that a mesh axis runs over, the one named last changes fastest.
Arguments:
- phases: float32 [128, 16, 256], P(('slab', 'xsec')), may hold values from -3.140625 to 3.140625
- onsite: bfloat16 [128, 256, 256], P(('slab', 'xsec')), may hold values from -0.375 to 0.375
- coupling: bfloat16 [128, 256, 256], P(('slab', 'xsec')), may hold values from -0.375 to 0.375
- pair_blocks: bfloat16 [768, 256, 256], P(('slab', 'xsec')), may hold values from -0.375 to 0.375
- pair_source: int32 [768], P(('slab', 'xsec')), may hold values from 0 to 3
- pair_partner: int32 [768], P(('slab', 'xsec')), may hold values from 0 to 31, as said below
Outputs:
- first: float32 [128, 16, 256], P(('slab', 'xsec'))
- second: float32 [128, 16, 256], P(('slab', 'xsec'))
The draws below stay inside these ranges and needn't reach their ends.
Inputs may be any that keep to these rules, and one draw needn't show every extreme that they name: `pair_partner`: the stored blocks of one device name at most 6 partner clusters on any one device of the slab, and exactly 6 on some device.
All inputs are finite; a program needn't handle non-finite values.
Results may differ from the reference program's by a relative error of at most 0.0043.
Values may be sent and summed in bfloat16 or wider, within the bound.
A program may use at most 64 MiB of HBM per device.

```python
import math
import jax
import jax.numpy as jnp
from jax import lax

ORB = 256
PROBES = 16
CL_DEV = 4
PAIR_PER = 6
PAIRS_DEV = 24
CAP = 6
SLAB_CLUSTERS = 32
CLUSTERS = 128
PAIRS = 768
N_SLAB = 4
N_XSEC = 8


def draw_pair_partner(key, part):
    slot_total = N_XSEC * CAP
    shared = jax.random.randint(jax.random.fold_in(key, 7), (N_XSEC,), 0, 1 << 19)

    def one_device(device_key):
        key_full, key_score, key_local = jax.random.split(device_key, 3)
        full_peer = jax.random.randint(key_full, (), 0, N_XSEC)
        slot_ids = jnp.arange(slot_total, dtype=jnp.int32)
        peers = slot_ids // CAP
        scores = jax.random.randint(key_score, (slot_total,), 0, 1 << 19) + shared[peers]
        scores = jnp.where(peers == full_peer, -1, scores) * slot_total + slot_ids
        order = jnp.argsort(scores, stable=True)
        chosen = peers[order[:PAIRS_DEV]]
        local = jax.random.randint(key_local, (PAIRS_DEV,), 0, CL_DEV)
        return (chosen * CL_DEV + local).astype(jnp.int32)
    keys = jax.random.split(key, N_SLAB * N_XSEC)
    return jax.vmap(one_device)(keys).reshape(-1)


def place_ends(entries, stream_key, smallest, top_value):
    extent = entries.shape
    place = [jax.random.randint(jax.random.fold_in(stream_key, axis), (), 0, extent[axis]) for axis in range(len(extent))]
    entries = entries.at[tuple(place)].set(smallest)
    longest = extent.index(max(extent))
    place[longest] = (place[longest] + 1) % extent[longest]
    return entries.at[tuple(place)].set(top_value)


def levels(own_key, extent, shards, smallest, largest):
    gain, own = 1.0, jax.random.fold_in(own_key, 6)
    for position, blocks in shards:
        heights = jnp.exp(jax.random.uniform(jax.random.fold_in(own, position), (blocks,), jnp.float32, smallest / len(shards), largest / len(shards)))
        gain = gain * jnp.repeat(heights, extent[position] // blocks).reshape([-1 if axis == position else 1 for axis in range(len(extent))])
    return gain


def gaussian(rng, shape, spread, bound, cuts=(), kind=jnp.bfloat16):
    values = spread * jax.random.normal(rng, shape, jnp.float32)
    if cuts:
        values = values * levels(rng, shape, cuts, -0.22, 0.18)
    return jnp.clip(values, -bound, bound).astype(kind)


def setup_inputs(seed: int = 0) -> dict:
    arg_keys = jax.random.split(jax.random.key(seed), 7)
    phases = jnp.clip(jax.random.uniform(arg_keys[0], (CLUSTERS, PROBES, ORB), jnp.float32, -3.140625, 3.140625), -3.140625, 3.140625)
    onsite = gaussian(arg_keys[1], (CLUSTERS, ORB, ORB), ORB ** -0.5, 0.375, ((0, 32),))
    coupling = gaussian(arg_keys[2], (CLUSTERS, ORB, ORB), ORB ** -0.5, 0.375, ((0, 32),))
    pair_blocks = gaussian(arg_keys[3], (PAIRS, ORB, ORB), ORB ** -0.5, 0.375, ((0, 32),))
    pair_source = place_ends(jax.random.randint(arg_keys[4], (PAIRS,), 0, CL_DEV), jax.random.fold_in(arg_keys[4], 1), 0, CL_DEV - 1).astype(jnp.int32)
    pair_partner = draw_pair_partner(jax.random.fold_in(arg_keys[6], 71), 0)
    return dict(phases=phases, onsite=onsite, coupling=coupling, pair_blocks=pair_blocks, pair_source=pair_source, pair_partner=pair_partner)


def block_terms(pieces):
    blocks, left, right = pieces
    wide = blocks.astype(jnp.float32)
    forward = jnp.einsum('nij,npj->npi', wide, right.astype(jnp.float32))
    backward = jnp.einsum('nji,npj->npi', wide, left.astype(jnp.float32))
    return (forward, backward)

def apply_hamiltonian(field, onsite, coupling, pair_blocks, source_index, partner_index):
    devices = N_SLAB * N_XSEC
    width = SLAB_CLUSTERS

    def per_device(array):
        return array.reshape((devices, -1) + array.shape[1:])
    shape = field.shape
    on_fwd, on_bwd = lax.map(block_terms, (per_device(onsite), per_device(field), per_device(field)))
    result = (0.5 * (on_fwd + on_bwd)).reshape(shape)
    upper = jnp.concatenate([field[width:], jnp.zeros_like(field[:width])], axis=0)
    cp_fwd, cp_bwd = lax.map(block_terms, (per_device(coupling), per_device(field), per_device(upper)))
    result = result + cp_fwd.reshape(shape)
    cp_bwd = cp_bwd.reshape(shape)
    result = result + jnp.concatenate([jnp.zeros((width,) + shape[1:], jnp.float32), cp_bwd[:-width]], axis=0)
    own_x = field[source_index]
    partner_x = field[partner_index]
    pr_fwd, pr_bwd = lax.map(block_terms, (per_device(pair_blocks), per_device(own_x), per_device(partner_x)))
    result = result.at[source_index].add(pr_fwd.reshape(own_x.shape))
    result = result.at[partner_index].add(pr_bwd.reshape(own_x.shape))
    return result * (1.0 / math.sqrt(3.0 + 2.0 * PAIR_PER))

def reference(phases, onsite, coupling, pair_blocks, pair_source, pair_partner):
    owner = jnp.arange(PAIRS, dtype=jnp.int32) // PAIRS_DEV
    slab_of = owner // N_XSEC
    source_index = (owner * CL_DEV + pair_source).astype(jnp.int32)
    partner_index = (slab_of * SLAB_CLUSTERS + pair_partner).astype(jnp.int32)
    start = math.sqrt(2.0) * jnp.cos(phases)
    first = apply_hamiltonian(start.astype(jnp.bfloat16), onsite, coupling, pair_blocks, source_index, partner_index)
    second = 2.0 * apply_hamiltonian(first.astype(jnp.bfloat16), onsite, coupling, pair_blocks, source_index, partner_index) - start
    return (first, second)
```

```python
import functools
import math

import jax
import jax.numpy as jnp
from jax import lax
from jax.experimental import pallas as pl
from jax.experimental.pallas import tpu as pltpu
from jax.sharding import PartitionSpec as P

F32 = jnp.float32
BF16 = jnp.bfloat16
CHUNKS = 4


def cosine(x):
    h = 0.5 * x
    square = h * h
    total = jnp.full_like(square, 1.0 / math.factorial(13))
    for order in (11, 9, 7, 5, 3, 1):
        sign = 1.0 if order % 4 == 1 else -1.0
        total = total * square + sign / math.factorial(order)
    sine = h * total
    return 1.0 - 2.0 * sine * sine


def plain(left, right):
    return lax.dot_general(left, right, (((1,), (0,)), ((), ())), preferred_element_type=F32)


def flipped(left, right):
    return lax.dot_general(left, right, (((1,), (1,)), ((), ())), preferred_element_type=F32)


def halves(value):
    high = value.astype(BF16)
    return high, (value - high.astype(F32)).astype(BF16)


def kernel(
    slabs, peers, clusters, pairs, probes, orb,
    partner_ref, source_ref, phases_hbm, onsite_hbm, coupling_hbm, pairs_hbm,
    first_ref, second_ref,
    onsite, coupling, blocks, phases, start, fields_0, fields_1, own, above, going, coming, down_out, down_in,
    spread, collect, products_high, products_low,
    load_sem, field_send, field_recv, prod_send, prod_recv, up_send, up_recv, down_send, down_recv,
):
    slab = lax.axis_index("slab")
    me = lax.axis_index("xsec")
    rows = clusters * probes
    factor = 1.0 / math.sqrt(3.0 + 2.0 * pairs / clusters)
    part = pairs // CHUNKS
    fields = (fields_0, fields_1)

    loads = [
        pltpu.make_async_copy(phases_hbm, phases, load_sem.at[2 + CHUNKS]),
        pltpu.make_async_copy(coupling_hbm, coupling, load_sem.at[0]),
    ]
    for chunk in range(CHUNKS):
        span = pl.ds(chunk * part, part)
        loads.append(
            pltpu.make_async_copy(pairs_hbm.at[span], blocks.at[span], load_sem.at[1 + chunk])
        )
    loads.append(pltpu.make_async_copy(onsite_hbm, onsite, load_sem.at[1 + CHUNKS]))
    for load in loads:
        load.start()
    phases_load, loads = loads[0], loads[1:]

    def peer(offset):
        return lax.rem(me + offset, peers)

    barrier = pltpu.get_barrier_semaphore()
    for offset in range(1, peers):
        pl.semaphore_signal(
            barrier, inc=1, device_id=(slab, peer(offset)), device_id_type=pl.DeviceIdType.MESH
        )

    @pl.when(slab > 0)
    def _():
        pl.semaphore_signal(
            barrier, inc=1, device_id=(slab - 1, me), device_id_type=pl.DeviceIdType.MESH
        )

    @pl.when(slab < slabs - 1)
    def _():
        pl.semaphore_signal(
            barrier, inc=1, device_id=(slab + 1, me), device_id_type=pl.DeviceIdType.MESH
        )

    phases_load.wait()
    begin = math.sqrt(2.0) * cosine(phases[...]).reshape(rows, orb)
    start[...] = begin

    width = pairs * probes
    lane = lax.broadcasted_iota(jnp.int32, (1, width), 1)
    group = lane // probes
    inner = lane % probes
    partner_row = jnp.zeros((1, width), jnp.int32)
    source_row = jnp.zeros((1, width), jnp.int32)
    for k in range(pairs):
        partner_row = jnp.where(group == k, partner_ref[k], partner_row)
        source_row = jnp.where(group == k, source_ref[k], source_row)
    partner_row = partner_row * probes + inner
    source_row = source_row * probes + inner

    neighbours = (slab > 0).astype(jnp.int32) + (slab < slabs - 1).astype(jnp.int32)
    pl.semaphore_wait(barrier, peers - 1 + neighbours)

    def field_copy(step, offset):
        span = fields[step].at[pl.ds(me * clusters, clusters)]
        return pltpu.make_async_remote_copy(
            src_ref=span, dst_ref=span,
            send_sem=field_send.at[step, offset], recv_sem=field_recv.at[step, offset],
            device_id=(slab, peer(offset)), device_id_type=pl.DeviceIdType.MESH,
        )

    def product_copy(step, offset):
        return pltpu.make_async_remote_copy(
            src_ref=going.at[step, pl.ds(peer(offset) * rows, rows)],
            dst_ref=coming.at[step, offset],
            send_sem=prod_send.at[step, offset], recv_sem=prod_recv.at[step, offset],
            device_id=(slab, peer(offset)), device_id_type=pl.DeviceIdType.MESH,
        )

    def up_copy(step):
        return pltpu.make_async_remote_copy(
            src_ref=own.at[step], dst_ref=above.at[step],
            send_sem=up_send.at[step], recv_sem=up_recv.at[step],
            device_id=(slab - 1, me), device_id_type=pl.DeviceIdType.MESH,
        )

    def down_copy(step):
        return pltpu.make_async_remote_copy(
            src_ref=down_out.at[step], dst_ref=down_in.at[step],
            send_sem=down_send.at[step], recv_sem=down_recv.at[step],
            device_id=(slab + 1, me), device_id_type=pl.DeviceIdType.MESH,
        )

    def keep(k, value):
        high, low = halves(value)
        products_high[pl.ds(k * probes, probes)] = high
        products_low[pl.ds(k * probes, probes)] = low

    def apply_field(step, value):
        field = value.astype(BF16).reshape(clusters, probes, orb)
        own[step] = field
        fields[step][pl.ds(me * clusters, clusters)] = field
        for offset in range(1, peers):
            field_copy(step, offset).start()

        @pl.when(slab > 0)
        def _():
            up_copy(step).start()

        if step == 0:
            spread_rows = lax.broadcasted_iota(jnp.int32, spread.shape, 0)
            spread[...] = (spread_rows == partner_row).astype(F32).astype(BF16)
            collect_rows = lax.broadcasted_iota(jnp.int32, collect.shape, 0)
            collect[...] = (collect_rows == source_row).astype(F32).astype(BF16)
            loads[0].wait()
        for c in range(clusters):
            down_out[step, pl.ds(c * probes, probes)] = plain(field[c], coupling[c])

        @pl.when(slab < slabs - 1)
        def _():
            down_copy(step).start()

        for k in range(pairs):
            if step == 0 and k % part == 0:
                loads[1 + k // part].wait()
            keep(k, plain(own[step, source_ref[k]], blocks[k]))
        high = products_high[...]
        low = products_low[...]
        going[step] = (plain(spread[...], high) + plain(spread[...], low)).astype(BF16)
        for offset in range(1, peers):
            product_copy(step, offset).start()

        if step == 0:
            loads[1 + CHUNKS].wait()
        local = []
        for c in range(clusters):
            local.append(0.5 * (plain(field[c], onsite[c]) + flipped(field[c], onsite[c])))
        result = jnp.concatenate(local, axis=0)

        for offset in range(1, peers):
            field_copy(step, offset).wait_recv()
        for k in range(pairs):
            keep(k, flipped(fields[step][partner_ref[k]], blocks[k]))
        high = products_high[...]
        low = products_low[...]
        result = result + (plain(collect[...], high) + plain(collect[...], low))

        @pl.when(slab < slabs - 1)
        def _():
            up_copy(step).wait_recv()

        @pl.when(slab == slabs - 1)
        def _():
            above[step] = jnp.zeros_like(own[step])

        result = result + jnp.concatenate(
            [flipped(above[step, c], coupling[c]) for c in range(clusters)], axis=0
        )

        @pl.when(slab > 0)
        def _():
            down_copy(step).wait_recv()

        @pl.when(slab == 0)
        def _():
            down_in[step] = jnp.zeros_like(start)

        result = result + down_in[step]
        result = result + going[step, pl.ds(me * rows, rows)].astype(F32)
        for offset in range(1, peers):
            product_copy(step, offset).wait_recv()
            result = result + coming[step, offset].astype(F32)
        return result * factor

    first = apply_field(0, begin)
    first_ref[...] = first.reshape(clusters, probes, orb)
    second = 2.0 * apply_field(1, first) - start[...]
    second_ref[...] = second.reshape(clusters, probes, orb)

    for step in range(2):
        for offset in range(1, peers):
            field_copy(step, offset).wait_send()
            product_copy(step, offset).wait_send()

        @pl.when(slab > 0)
        def _():
            up_copy(step).wait_send()

        @pl.when(slab < slabs - 1)
        def _():
            down_copy(step).wait_send()


def per_device(phases, onsite, coupling, pair_blocks, pair_source, pair_partner):
    clusters, probes, orb = phases.shape
    pairs = pair_blocks.shape[0]
    slabs = lax.axis_size("slab")
    peers = lax.axis_size("xsec")
    slots = peers * clusters
    rows = clusters * probes
    vmem = pl.BlockSpec(memory_space=pltpu.VMEM)
    smem = pl.BlockSpec(memory_space=pltpu.SMEM)
    hbm = pl.BlockSpec(memory_space=pltpu.HBM)
    dma = pltpu.SemaphoreType.DMA
    out = jax.ShapeDtypeStruct(phases.shape, F32)
    return pl.pallas_call(
        functools.partial(kernel, slabs, peers, clusters, pairs, probes, orb),
        out_shape=(out, out),
        in_specs=[smem, smem, hbm, hbm, hbm, hbm],
        out_specs=(vmem, vmem),
        scratch_shapes=[
            pltpu.VMEM((clusters, orb, orb), BF16),
            pltpu.VMEM((clusters, orb, orb), BF16),
            pltpu.VMEM((pairs, orb, orb), BF16),
            pltpu.VMEM((clusters, probes, orb), F32),
            pltpu.VMEM((rows, orb), F32),
            pltpu.VMEM((slots, probes, orb), BF16),
            pltpu.VMEM((slots, probes, orb), BF16),
            pltpu.VMEM((2, clusters, probes, orb), BF16),
            pltpu.VMEM((2, clusters, probes, orb), BF16),
            pltpu.VMEM((2, slots * probes, orb), BF16),
            pltpu.VMEM((2, peers, rows, orb), BF16),
            pltpu.VMEM((2, rows, orb), F32),
            pltpu.VMEM((2, rows, orb), F32),
            pltpu.VMEM((slots * probes, pairs * probes), BF16),
            pltpu.VMEM((rows, pairs * probes), BF16),
            pltpu.VMEM((pairs * probes, orb), BF16),
            pltpu.VMEM((pairs * probes, orb), BF16),
            dma((3 + CHUNKS,)),
            dma((2, peers)), dma((2, peers)), dma((2, peers)), dma((2, peers)),
            dma((2,)), dma((2,)), dma((2,)), dma((2,)),
        ],
        compiler_params=pltpu.CompilerParams(
            collective_id=0, has_side_effects=True, vmem_limit_bytes=63 * 1024 * 1024
        ),
    )(pair_partner, pair_source, phases, onsite, coupling, pair_blocks)


def solution(mesh):
    spec = P(("slab", "xsec"), None, None)
    flat = P(("slab", "xsec"))
    return jax.shard_map(
        per_device,
        mesh=mesh,
        in_specs=(spec, spec, spec, spec, flat, flat),
        out_specs=(spec, spec),
        check_vma=False,
    )
```

```python
import functools
import math

import jax
import jax.numpy as jnp
from jax import lax
from jax.experimental import pallas as pl
from jax.experimental.pallas import tpu as pltpu
from jax.sharding import PartitionSpec as P

F32 = jnp.float32
BF16 = jnp.bfloat16
CHUNKS = 4


def cosine(x):
    h = 0.5 * x
    square = h * h
    total = jnp.full_like(square, 1.0 / math.factorial(13))
    for order in (11, 9, 7, 5, 3, 1):
        sign = 1.0 if order % 4 == 1 else -1.0
        total = total * square + sign / math.factorial(order)
    sine = h * total
    return 1.0 - 2.0 * sine * sine


def plain(left, right):
    return lax.dot_general(left, right, (((1,), (0,)), ((), ())), preferred_element_type=F32)


def flipped(left, right):
    return lax.dot_general(left, right, (((1,), (1,)), ((), ())), preferred_element_type=F32)


def halves(value):
    high = value.astype(BF16)
    return high, (value - high.astype(F32)).astype(BF16)


def kernel(
    slabs, peers, clusters, pairs, probes, orb,
    partner_ref, source_ref, phases_hbm, onsite_hbm, coupling_hbm, pairs_hbm,
    first_ref, second_ref,
    onsite, coupling, blocks, phases, start, fields_0, fields_1, own, above, going, traded, leaving, coming, down_out, down_in,
    spread, collect, products_high, products_low,
    load_sem, field_send, field_recv, hand_send, hand_recv, trade_send, trade_recv, prod_send, prod_recv,
    up_send, up_recv, down_send, down_recv,
):
    slab = lax.axis_index("slab")
    me = lax.axis_index("xsec")
    rows = clusters * probes
    factor = 1.0 / math.sqrt(3.0 + 2.0 * pairs / clusters)
    part = pairs // CHUNKS
    fields = (fields_0, fields_1)

    loads = [
        pltpu.make_async_copy(phases_hbm, phases, load_sem.at[2 + CHUNKS]),
        pltpu.make_async_copy(coupling_hbm, coupling, load_sem.at[0]),
    ]
    for chunk in range(CHUNKS):
        span = pl.ds(chunk * part, part)
        loads.append(
            pltpu.make_async_copy(pairs_hbm.at[span], blocks.at[span], load_sem.at[1 + chunk])
        )
    loads.append(pltpu.make_async_copy(onsite_hbm, onsite, load_sem.at[1 + CHUNKS]))
    for load in loads:
        load.start()
    phases_load, loads = loads[0], loads[1:]

    chips = peers // 2
    chip = me // 2
    core = lax.rem(me, 2)
    sibling = me + 1 - 2 * core

    def peer(offset):
        return lax.rem(chip + offset, chips) * 2 + core

    def origin(offset):
        return lax.rem(chip - offset + chips, chips) * 2 + core

    far = list(range(chips - 1, 0, -1))
    barrier = pltpu.get_barrier_semaphore()
    for offset in far:
        pl.semaphore_signal(
            barrier, inc=1, device_id=(slab, peer(offset)), device_id_type=pl.DeviceIdType.MESH
        )
    pl.semaphore_signal(
        barrier, inc=1, device_id=(slab, sibling), device_id_type=pl.DeviceIdType.MESH
    )

    @pl.when(slab > 0)
    def _():
        pl.semaphore_signal(
            barrier, inc=1, device_id=(slab - 1, me), device_id_type=pl.DeviceIdType.MESH
        )

    @pl.when(slab < slabs - 1)
    def _():
        pl.semaphore_signal(
            barrier, inc=1, device_id=(slab + 1, me), device_id_type=pl.DeviceIdType.MESH
        )

    phases_load.wait()
    begin = math.sqrt(2.0) * cosine(phases[...]).reshape(rows, orb)
    start[...] = begin

    width = pairs * probes
    lane = lax.broadcasted_iota(jnp.int32, (1, width), 1)
    group = lane // probes
    inner = lane % probes
    partner_row = jnp.zeros((1, width), jnp.int32)
    source_row = jnp.zeros((1, width), jnp.int32)
    for k in range(pairs):
        partner_row = jnp.where(group == k, partner_ref[k], partner_row)
        source_row = jnp.where(group == k, source_ref[k], source_row)
    partner_row = partner_row * probes + inner
    source_row = source_row * probes + inner

    neighbours = (slab > 0).astype(jnp.int32) + (slab < slabs - 1).astype(jnp.int32)
    pl.semaphore_wait(barrier, chips + neighbours)

    def field_copy(step, offset):
        span = fields[step].at[pl.ds(me * clusters, clusters)]
        return pltpu.make_async_remote_copy(
            src_ref=span, dst_ref=span,
            send_sem=field_send.at[step, offset], recv_sem=field_recv.at[step, offset],
            device_id=(slab, peer(offset) if offset else sibling),
            device_id_type=pl.DeviceIdType.MESH,
        )

    def handed_copy(step, offset):
        span = fields[step].at[pl.ds(origin(offset) * clusters, clusters)]
        return pltpu.make_async_remote_copy(
            src_ref=span, dst_ref=span,
            send_sem=hand_send.at[step, offset], recv_sem=hand_recv.at[step, offset],
            device_id=(slab, sibling), device_id_type=pl.DeviceIdType.MESH,
        )

    def exchange_copy(step, offset):
        target = lax.rem(chip + offset, chips) * 2 + 1 - core
        return pltpu.make_async_remote_copy(
            src_ref=going.at[step, pl.ds(target * rows, rows)],
            dst_ref=traded.at[step, offset],
            send_sem=trade_send.at[step, offset], recv_sem=trade_recv.at[step, offset],
            device_id=(slab, sibling), device_id_type=pl.DeviceIdType.MESH,
        )

    def product_copy(step, offset):
        return pltpu.make_async_remote_copy(
            src_ref=leaving.at[step, offset], dst_ref=coming.at[step, offset],
            send_sem=prod_send.at[step, offset], recv_sem=prod_recv.at[step, offset],
            device_id=(slab, peer(offset)), device_id_type=pl.DeviceIdType.MESH,
        )

    def up_copy(step):
        return pltpu.make_async_remote_copy(
            src_ref=own.at[step], dst_ref=above.at[step],
            send_sem=up_send.at[step], recv_sem=up_recv.at[step],
            device_id=(slab - 1, me), device_id_type=pl.DeviceIdType.MESH,
        )

    def down_copy(step):
        return pltpu.make_async_remote_copy(
            src_ref=down_out.at[step], dst_ref=down_in.at[step],
            send_sem=down_send.at[step], recv_sem=down_recv.at[step],
            device_id=(slab + 1, me), device_id_type=pl.DeviceIdType.MESH,
        )

    def keep(k, value):
        high, low = halves(value)
        products_high[pl.ds(k * probes, probes)] = high
        products_low[pl.ds(k * probes, probes)] = low

    def apply_field(step, value):
        field = value.astype(BF16).reshape(clusters, probes, orb)
        own[step] = field
        fields[step][pl.ds(me * clusters, clusters)] = field
        for offset in far + [0]:
            field_copy(step, offset).start()

        @pl.when(slab > 0)
        def _():
            up_copy(step).start()

        if step == 0:
            spread_rows = lax.broadcasted_iota(jnp.int32, spread.shape, 0)
            spread[...] = (spread_rows == partner_row).astype(F32).astype(BF16)
            collect_rows = lax.broadcasted_iota(jnp.int32, collect.shape, 0)
            collect[...] = (collect_rows == source_row).astype(F32).astype(BF16)
        for k in range(pairs):
            if step == 0 and k % part == 0:
                loads[1 + k // part].wait()
            keep(k, plain(own[step, source_ref[k]], blocks[k]))
        high = products_high[...]
        low = products_low[...]
        going[step] = plain(spread[...], high) + plain(spread[...], low)
        for offset in far + [0]:
            exchange_copy(step, offset).start()

        if step == 0:
            loads[0].wait()
        for c in range(clusters):
            down_out[step, pl.ds(c * probes, probes)] = plain(field[c], coupling[c])

        @pl.when(slab < slabs - 1)
        def _():
            down_copy(step).start()

        if step == 0:
            loads[1 + CHUNKS].wait()
        local = []
        for c in range(clusters):
            local.append(0.5 * (plain(field[c], onsite[c]) + flipped(field[c], onsite[c])))
        result = jnp.concatenate(local, axis=0)

        for offset in far:
            exchange_copy(step, offset).wait_recv()
            mine = going[step, pl.ds(peer(offset) * rows, rows)]
            leaving[step, offset] = (mine + traded[step, offset]).astype(BF16)
            product_copy(step, offset).start()
        for offset in far[::-1]:
            field_copy(step, offset).wait_recv()
            handed_copy(step, offset).start()
        field_copy(step, 0).wait_recv()
        exchange_copy(step, 0).wait_recv()
        result = result + going[step, pl.ds(me * rows, rows)] + traded[step, 0]

        @pl.when(slab < slabs - 1)
        def _():
            up_copy(step).wait_recv()

        @pl.when(slab == slabs - 1)
        def _():
            above[step] = jnp.zeros_like(own[step])

        result = result + jnp.concatenate(
            [flipped(above[step, c], coupling[c]) for c in range(clusters)], axis=0
        )

        @pl.when(slab > 0)
        def _():
            down_copy(step).wait_recv()

        @pl.when(slab == 0)
        def _():
            down_in[step] = jnp.zeros_like(start)

        result = result + down_in[step]
        for offset in far:
            handed_copy(step, offset).wait_recv()
        for k in range(pairs):
            keep(k, flipped(fields[step][partner_ref[k]], blocks[k]))
        high = products_high[...]
        low = products_low[...]
        result = result + (plain(collect[...], high) + plain(collect[...], low))
        for offset in far:
            product_copy(step, offset).wait_recv()
            result = result + coming[step, offset].astype(F32)
        return result * factor

    first = apply_field(0, begin)
    first_ref[...] = 0.5 * first.reshape(clusters, probes, orb)
    second = 2.0 * apply_field(1, first) - start[...]
    second_ref[...] = 0.5 * second.reshape(clusters, probes, orb)

    for step in range(2):
        for offset in range(chips):
            field_copy(step, offset).wait_send()
            exchange_copy(step, offset).wait_send()
        for offset in far:
            handed_copy(step, offset).wait_send()
            product_copy(step, offset).wait_send()

        @pl.when(slab > 0)
        def _():
            up_copy(step).wait_send()

        @pl.when(slab < slabs - 1)
        def _():
            down_copy(step).wait_send()


def per_device(phases, onsite, coupling, pair_blocks, pair_source, pair_partner):
    clusters, probes, orb = phases.shape
    pairs = pair_blocks.shape[0]
    slabs = lax.axis_size("slab")
    peers = lax.axis_size("xsec")
    slots = peers * clusters
    rows = clusters * probes
    vmem = pl.BlockSpec(memory_space=pltpu.VMEM)
    smem = pl.BlockSpec(memory_space=pltpu.SMEM)
    hbm = pl.BlockSpec(memory_space=pltpu.HBM)
    dma = pltpu.SemaphoreType.DMA
    out = jax.ShapeDtypeStruct(phases.shape, F32)
    raw = pl.pallas_call(
        functools.partial(kernel, slabs, peers, clusters, pairs, probes, orb),
        out_shape=(out, out),
        in_specs=[smem, smem, hbm, hbm, hbm, hbm],
        out_specs=(vmem, vmem),
        scratch_shapes=[
            pltpu.VMEM((clusters, orb, orb), BF16),
            pltpu.VMEM((clusters, orb, orb), BF16),
            pltpu.VMEM((pairs, orb, orb), BF16),
            pltpu.VMEM((clusters, probes, orb), F32),
            pltpu.VMEM((rows, orb), F32),
            pltpu.VMEM((slots, probes, orb), BF16),
            pltpu.VMEM((slots, probes, orb), BF16),
            pltpu.VMEM((2, clusters, probes, orb), BF16),
            pltpu.VMEM((2, clusters, probes, orb), BF16),
            pltpu.VMEM((2, slots * probes, orb), F32),
            pltpu.VMEM((2, peers // 2, rows, orb), F32),
            pltpu.VMEM((2, peers // 2, rows, orb), BF16),
            pltpu.VMEM((2, peers // 2, rows, orb), BF16),
            pltpu.VMEM((2, rows, orb), F32),
            pltpu.VMEM((2, rows, orb), F32),
            pltpu.VMEM((slots * probes, pairs * probes), BF16),
            pltpu.VMEM((rows, pairs * probes), BF16),
            pltpu.VMEM((pairs * probes, orb), BF16),
            pltpu.VMEM((pairs * probes, orb), BF16),
            dma((3 + CHUNKS,)),
            *[dma((2, peers // 2)) for _ in range(8)],
            dma((2,)), dma((2,)), dma((2,)), dma((2,)),
        ],
        compiler_params=pltpu.CompilerParams(
            collective_id=0, has_side_effects=True, vmem_limit_bytes=63 * 1024 * 1024
        ),
    )(pair_partner, pair_source, phases, onsite, coupling, pair_blocks)
    return 2.0 * raw[0], 2.0 * raw[1]


def solution(mesh):
    spec = P(("slab", "xsec"), None, None)
    flat = P(("slab", "xsec"))
    return jax.shard_map(
        per_device,
        mesh=mesh,
        in_specs=(spec, spec, spec, spec, flat, flat),
        out_specs=(spec, spec),
        check_vma=False,
    )
```

```python
import functools
import math

import jax
import jax.numpy as jnp
from jax import lax
from jax.experimental import pallas as pl
from jax.experimental.pallas import tpu as pltpu
from jax.sharding import PartitionSpec as P

F32 = jnp.float32
BF16 = jnp.bfloat16
CHUNKS = 4


def cosine(x):
    h = 0.5 * x
    square = h * h
    total = jnp.full_like(square, 1.0 / math.factorial(13))
    for order in (11, 9, 7, 5, 3, 1):
        sign = 1.0 if order % 4 == 1 else -1.0
        total = total * square + sign / math.factorial(order)
    sine = h * total
    return 1.0 - 2.0 * sine * sine


def plain(left, right):
    return lax.dot_general(left, right, (((1,), (0,)), ((), ())), preferred_element_type=F32)


def flipped(left, right):
    return lax.dot_general(left, right, (((1,), (1,)), ((), ())), preferred_element_type=F32)


def halves(value):
    high = value.astype(BF16)
    return high, (value - high.astype(F32)).astype(BF16)


def kernel(
    slabs, peers, clusters, pairs, probes, orb,
    partner_ref, source_ref, phases_hbm, onsite_hbm, coupling_hbm, pairs_hbm,
    first_ref, second_ref,
    onsite, coupling, blocks, phases, start, fields_0, fields_1, own, above, going, giving, traded, leaving, coming, down_out, down_in,
    spread, collect, products_high, products_low,
    load_sem, field_send, field_recv, hand_send, hand_recv, trade_send, trade_recv, prod_send, prod_recv,
    up_send, up_recv, down_send, down_recv,
):
    slab = lax.axis_index("slab")
    me = lax.axis_index("xsec")
    rows = clusters * probes
    factor = 1.0 / math.sqrt(3.0 + 2.0 * pairs / clusters)
    part = pairs // CHUNKS
    fields = (fields_0, fields_1)

    loads = [
        pltpu.make_async_copy(phases_hbm, phases, load_sem.at[2 + CHUNKS]),
        pltpu.make_async_copy(coupling_hbm, coupling, load_sem.at[0]),
    ]
    for chunk in range(CHUNKS):
        span = pl.ds(chunk * part, part)
        loads.append(
            pltpu.make_async_copy(pairs_hbm.at[span], blocks.at[span], load_sem.at[1 + chunk])
        )
    loads.append(pltpu.make_async_copy(onsite_hbm, onsite, load_sem.at[1 + CHUNKS]))
    for load in loads:
        load.start()
    phases_load, loads = loads[0], loads[1:]

    chips = peers // 2
    chip = me // 2
    core = lax.rem(me, 2)
    sibling = me + 1 - 2 * core

    def peer(offset):
        return lax.rem(chip + offset, chips) * 2 + core

    def origin(offset):
        return lax.rem(chip - offset + chips, chips) * 2 + core

    far = list(range(chips - 1, 0, -1))
    barrier = pltpu.get_barrier_semaphore()
    for offset in far:
        pl.semaphore_signal(
            barrier, inc=1, device_id=(slab, peer(offset)), device_id_type=pl.DeviceIdType.MESH
        )
    pl.semaphore_signal(
        barrier, inc=1, device_id=(slab, sibling), device_id_type=pl.DeviceIdType.MESH
    )

    @pl.when(slab > 0)
    def _():
        pl.semaphore_signal(
            barrier, inc=1, device_id=(slab - 1, me), device_id_type=pl.DeviceIdType.MESH
        )

    @pl.when(slab < slabs - 1)
    def _():
        pl.semaphore_signal(
            barrier, inc=1, device_id=(slab + 1, me), device_id_type=pl.DeviceIdType.MESH
        )

    phases_load.wait()
    begin = math.sqrt(2.0) * cosine(phases[...]).reshape(rows, orb)
    start[...] = begin

    width = pairs * probes
    half = chips * rows
    lane = lax.broadcasted_iota(jnp.int32, (1, width), 1)
    group = lane // probes
    inner = lane % probes
    partner_row = jnp.zeros((1, width), jnp.int32)
    source_row = jnp.zeros((1, width), jnp.int32)
    for k in range(pairs):
        partner_row = jnp.where(group == k, partner_ref[k], partner_row)
        source_row = jnp.where(group == k, source_ref[k], source_row)
    device = partner_row // clusters
    partner_row = (
        lax.rem(device, 2) * (half // probes) + device // 2 * clusters + lax.rem(partner_row, clusters)
    )
    partner_row = partner_row * probes + inner
    source_row = source_row * probes + inner

    def field_copy(step, offset):
        span = fields[step].at[pl.ds(me * clusters, clusters)]
        return pltpu.make_async_remote_copy(
            src_ref=span, dst_ref=span,
            send_sem=field_send.at[step, offset], recv_sem=field_recv.at[step, offset],
            device_id=(slab, peer(offset) if offset else sibling),
            device_id_type=pl.DeviceIdType.MESH,
        )

    def handed_copy(step, offset):
        span = fields[step].at[pl.ds(origin(offset) * clusters, clusters)]
        return pltpu.make_async_remote_copy(
            src_ref=span, dst_ref=span,
            send_sem=hand_send.at[step, offset], recv_sem=hand_recv.at[step, offset],
            device_id=(slab, sibling), device_id_type=pl.DeviceIdType.MESH,
        )

    def exchange_copy(step, offset):
        target = lax.rem(chip + offset, chips)
        return pltpu.make_async_remote_copy(
            src_ref=giving.at[step, pl.ds(target * rows, rows)],
            dst_ref=traded.at[step, offset],
            send_sem=trade_send.at[step, offset], recv_sem=trade_recv.at[step, offset],
            device_id=(slab, sibling), device_id_type=pl.DeviceIdType.MESH,
        )

    def product_copy(step, offset):
        return pltpu.make_async_remote_copy(
            src_ref=leaving.at[step, offset], dst_ref=coming.at[step, offset],
            send_sem=prod_send.at[step, offset], recv_sem=prod_recv.at[step, offset],
            device_id=(slab, peer(offset)), device_id_type=pl.DeviceIdType.MESH,
        )

    def up_copy(step):
        return pltpu.make_async_remote_copy(
            src_ref=own.at[step], dst_ref=above.at[step],
            send_sem=up_send.at[step], recv_sem=up_recv.at[step],
            device_id=(slab - 1, me), device_id_type=pl.DeviceIdType.MESH,
        )

    def down_copy(step):
        return pltpu.make_async_remote_copy(
            src_ref=down_out.at[step], dst_ref=down_in.at[step],
            send_sem=down_send.at[step], recv_sem=down_recv.at[step],
            device_id=(slab + 1, me), device_id_type=pl.DeviceIdType.MESH,
        )

    def keep(k, value):
        high, low = halves(value)
        products_high[pl.ds(k * probes, probes)] = high
        products_low[pl.ds(k * probes, probes)] = low

    def apply_field(step, value):
        field = value.astype(BF16).reshape(clusters, probes, orb)
        own[step] = field
        fields[step][pl.ds(me * clusters, clusters)] = field

        def send_fields():
            for offset in far + [0]:
                field_copy(step, offset).start()

            @pl.when(slab > 0)
            def _():
                up_copy(step).start()

        def send_down():
            @pl.when(slab < slabs - 1)
            def _():
                down_copy(step).start()

        def send_exchange():
            for offset in far + [0]:
                exchange_copy(step, offset).start()

        if step == 0:
            neighbours = (slab > 0).astype(jnp.int32) + (slab < slabs - 1).astype(jnp.int32)
            pl.semaphore_wait(barrier, chips + neighbours)
        send_fields()
        if step == 0:
            spread_rows = lax.broadcasted_iota(jnp.int32, spread.shape, 0)
            spread[...] = (spread_rows == partner_row).astype(F32).astype(BF16)
            collect_rows = lax.broadcasted_iota(jnp.int32, collect.shape, 0)
            collect[...] = (collect_rows == source_row).astype(F32).astype(BF16)
        for k in range(pairs):
            if step == 0 and k % part == 0:
                loads[1 + k // part].wait()
            keep(k, plain(own[step, source_ref[k]], blocks[k]))
        high = products_high[...]
        low = products_low[...]
        other = spread[pl.ds((1 - core) * half, half)]
        giving[step] = (plain(other, high) + plain(other, low)).astype(BF16)
        send_exchange()
        if step == 0:
            loads[0].wait()
        for c in range(clusters):
            down_out[step, pl.ds(c * probes, probes)] = plain(field[c], coupling[c]).astype(BF16)
        send_down()
        same = spread[pl.ds(core * half, half)]
        going[step] = plain(same, high) + plain(same, low)

        if step == 0:
            loads[1 + CHUNKS].wait()
        local = []
        for c in range(clusters):
            local.append(0.5 * (plain(field[c], onsite[c]) + flipped(field[c], onsite[c])))
        result = jnp.concatenate(local, axis=0)

        for offset in far:
            exchange_copy(step, offset).wait_recv()
            mine = going[step, pl.ds(lax.rem(chip + offset, chips) * rows, rows)]
            leaving[step, offset] = (mine + traded[step, offset].astype(F32)).astype(BF16)
            product_copy(step, offset).start()
        for offset in far[::-1]:
            field_copy(step, offset).wait_recv()
            handed_copy(step, offset).start()
        field_copy(step, 0).wait_recv()
        exchange_copy(step, 0).wait_recv()
        result = result + going[step, pl.ds(chip * rows, rows)] + traded[step, 0].astype(F32)

        @pl.when(slab < slabs - 1)
        def _():
            up_copy(step).wait_recv()

        @pl.when(slab == slabs - 1)
        def _():
            above[step] = jnp.zeros_like(own[step])

        result = result + jnp.concatenate(
            [flipped(above[step, c], coupling[c]) for c in range(clusters)], axis=0
        )

        @pl.when(slab > 0)
        def _():
            down_copy(step).wait_recv()

        @pl.when(slab == 0)
        def _():
            down_in[step] = jnp.zeros(start.shape, BF16)

        result = result + down_in[step].astype(F32)
        for offset in far:
            handed_copy(step, offset).wait_recv()
        for k in range(pairs):
            keep(k, flipped(fields[step][partner_ref[k]], blocks[k]))
        high = products_high[...]
        low = products_low[...]
        result = result + (plain(collect[...], high) + plain(collect[...], low))
        for offset in far:
            product_copy(step, offset).wait_recv()
            result = result + coming[step, offset].astype(F32)
        return result * factor

    first = apply_field(0, begin)
    first_ref[...] = 0.5 * first.reshape(clusters, probes, orb)
    second = 2.0 * apply_field(1, first) - start[...]
    second_ref[...] = 0.5 * second.reshape(clusters, probes, orb)

    for step in range(2):
        for offset in range(chips):
            field_copy(step, offset).wait_send()
            exchange_copy(step, offset).wait_send()
        for offset in far:
            handed_copy(step, offset).wait_send()
            product_copy(step, offset).wait_send()

        @pl.when(slab > 0)
        def _():
            up_copy(step).wait_send()

        @pl.when(slab < slabs - 1)
        def _():
            down_copy(step).wait_send()


def per_device(phases, onsite, coupling, pair_blocks, pair_source, pair_partner):
    clusters, probes, orb = phases.shape
    pairs = pair_blocks.shape[0]
    slabs = lax.axis_size("slab")
    peers = lax.axis_size("xsec")
    slots = peers * clusters
    rows = clusters * probes
    vmem = pl.BlockSpec(memory_space=pltpu.VMEM)
    smem = pl.BlockSpec(memory_space=pltpu.SMEM)
    hbm = pl.BlockSpec(memory_space=pltpu.HBM)
    dma = pltpu.SemaphoreType.DMA
    out = jax.ShapeDtypeStruct(phases.shape, F32)
    raw = pl.pallas_call(
        functools.partial(kernel, slabs, peers, clusters, pairs, probes, orb),
        out_shape=(out, out),
        in_specs=[smem, smem, hbm, hbm, hbm, hbm],
        out_specs=(vmem, vmem),
        scratch_shapes=[
            pltpu.VMEM((clusters, orb, orb), BF16),
            pltpu.VMEM((clusters, orb, orb), BF16),
            pltpu.VMEM((pairs, orb, orb), BF16),
            pltpu.VMEM((clusters, probes, orb), F32),
            pltpu.VMEM((rows, orb), F32),
            pltpu.VMEM((slots, probes, orb), BF16),
            pltpu.VMEM((slots, probes, orb), BF16),
            pltpu.VMEM((2, clusters, probes, orb), BF16),
            pltpu.VMEM((2, clusters, probes, orb), BF16),
            pltpu.VMEM((2, slots * probes // 2, orb), F32),
            pltpu.VMEM((2, slots * probes // 2, orb), BF16),
            pltpu.VMEM((2, peers // 2, rows, orb), BF16),
            pltpu.VMEM((2, peers // 2, rows, orb), BF16),
            pltpu.VMEM((2, peers // 2, rows, orb), BF16),
            pltpu.VMEM((2, rows, orb), BF16),
            pltpu.VMEM((2, rows, orb), BF16),
            pltpu.VMEM((slots * probes, pairs * probes), BF16),
            pltpu.VMEM((rows, pairs * probes), BF16),
            pltpu.VMEM((pairs * probes, orb), BF16),
            pltpu.VMEM((pairs * probes, orb), BF16),
            dma((3 + CHUNKS,)),
            *[dma((2, peers // 2)) for _ in range(8)],
            dma((2,)), dma((2,)), dma((2,)), dma((2,)),
        ],
        compiler_params=pltpu.CompilerParams(
            collective_id=0, has_side_effects=True, vmem_limit_bytes=63 * 1024 * 1024
        ),
    )(pair_partner, pair_source, phases, onsite, coupling, pair_blocks)
    return 2.0 * raw[0], 2.0 * raw[1]


def solution(mesh):
    spec = P(("slab", "xsec"), None, None)
    flat = P(("slab", "xsec"))
    return jax.shard_map(
        per_device,
        mesh=mesh,
        in_specs=(spec, spec, spec, spec, flat, flat),
        out_specs=(spec, spec),
        check_vma=False,
    )
```

```python
import functools
import math

import jax
import jax.numpy as jnp
from jax import lax
from jax.experimental import pallas as pl
from jax.experimental.pallas import tpu as pltpu
from jax.sharding import PartitionSpec as P

F32 = jnp.float32
BF16 = jnp.bfloat16
CHUNKS = 4


def cosine(x):
    h = 0.5 * x
    square = h * h
    total = jnp.full_like(square, 1.0 / math.factorial(13))
    for order in (11, 9, 7, 5, 3, 1):
        sign = 1.0 if order % 4 == 1 else -1.0
        total = total * square + sign / math.factorial(order)
    sine = h * total
    return 1.0 - 2.0 * sine * sine


def plain(left, right):
    return lax.dot_general(left, right, (((1,), (0,)), ((), ())), preferred_element_type=F32)


def flipped(left, right):
    return lax.dot_general(left, right, (((1,), (1,)), ((), ())), preferred_element_type=F32)


def halves(value):
    high = value.astype(BF16)
    return high, (value - high.astype(F32)).astype(BF16)


def kernel(
    slabs, peers, clusters, pairs, probes, orb,
    partner_ref, source_ref, phases_hbm, onsite_hbm, coupling_hbm, pairs_hbm,
    first_ref, second_ref,
    onsite, coupling, blocks, phases, start, fields_0, fields_1, own, above, going, giving, traded, leaving, coming, down_out, down_in,
    spread, collect, products_high, products_low,
    load_sem, field_send, field_recv, hand_send, hand_recv, trade_send, trade_recv, prod_send, prod_recv,
    up_send, up_recv, down_send, down_recv,
):
    slab = lax.axis_index("slab")
    me = lax.axis_index("xsec")
    rows = clusters * probes
    factor = 1.0 / math.sqrt(3.0 + 2.0 * pairs / clusters)
    part = pairs // CHUNKS
    fields = (fields_0, fields_1)

    loads = [
        pltpu.make_async_copy(phases_hbm, phases, load_sem.at[2 + CHUNKS]),
        pltpu.make_async_copy(coupling_hbm, coupling, load_sem.at[0]),
    ]
    for chunk in range(CHUNKS):
        span = pl.ds(chunk * part, part)
        loads.append(
            pltpu.make_async_copy(pairs_hbm.at[span], blocks.at[span], load_sem.at[1 + chunk])
        )
    loads.append(pltpu.make_async_copy(onsite_hbm, onsite, load_sem.at[1 + CHUNKS]))
    phases_load, loads = loads[0], loads[1:]
    phases_load.start()

    chips = peers // 2
    chip = me // 2
    core = lax.rem(me, 2)
    sibling = me + 1 - 2 * core

    def peer(offset):
        return lax.rem(chip + offset, chips) * 2 + core

    def origin(offset):
        return lax.rem(chip - offset + chips, chips) * 2 + core

    far = list(range(chips - 1, 0, -1))
    barrier = pltpu.get_barrier_semaphore()
    for offset in far:
        pl.semaphore_signal(
            barrier, inc=1, device_id=(slab, peer(offset)), device_id_type=pl.DeviceIdType.MESH
        )
    pl.semaphore_signal(
        barrier, inc=1, device_id=(slab, sibling), device_id_type=pl.DeviceIdType.MESH
    )

    @pl.when(slab > 0)
    def _():
        pl.semaphore_signal(
            barrier, inc=1, device_id=(slab - 1, me), device_id_type=pl.DeviceIdType.MESH
        )

    @pl.when(slab < slabs - 1)
    def _():
        pl.semaphore_signal(
            barrier, inc=1, device_id=(slab + 1, me), device_id_type=pl.DeviceIdType.MESH
        )

    for load in loads:
        load.start()
    phases_load.wait()
    begin = math.sqrt(2.0) * cosine(phases[...]).reshape(rows, orb)
    start[...] = begin

    width = pairs * probes
    half = chips * rows
    def field_copy(step, offset):
        span = fields[step].at[pl.ds(me * clusters, clusters)]
        return pltpu.make_async_remote_copy(
            src_ref=span, dst_ref=span,
            send_sem=field_send.at[step, offset], recv_sem=field_recv.at[step, offset],
            device_id=(slab, peer(offset) if offset else sibling),
            device_id_type=pl.DeviceIdType.MESH,
        )

    def handed_copy(step, offset):
        span = fields[step].at[pl.ds(origin(offset) * clusters, clusters)]
        return pltpu.make_async_remote_copy(
            src_ref=span, dst_ref=span,
            send_sem=hand_send.at[step, offset], recv_sem=hand_recv.at[step, offset],
            device_id=(slab, sibling), device_id_type=pl.DeviceIdType.MESH,
        )

    def exchange_copy(step, offset):
        target = lax.rem(chip + offset, chips)
        return pltpu.make_async_remote_copy(
            src_ref=giving.at[step, pl.ds(target * rows, rows)],
            dst_ref=traded.at[step, offset],
            send_sem=trade_send.at[step, offset], recv_sem=trade_recv.at[step, offset],
            device_id=(slab, sibling), device_id_type=pl.DeviceIdType.MESH,
        )

    def product_copy(step, offset):
        return pltpu.make_async_remote_copy(
            src_ref=leaving.at[step, offset], dst_ref=coming.at[step, offset],
            send_sem=prod_send.at[step, offset], recv_sem=prod_recv.at[step, offset],
            device_id=(slab, peer(offset)), device_id_type=pl.DeviceIdType.MESH,
        )

    def up_copy(step):
        return pltpu.make_async_remote_copy(
            src_ref=own.at[step], dst_ref=above.at[step],
            send_sem=up_send.at[step], recv_sem=up_recv.at[step],
            device_id=(slab - 1, me), device_id_type=pl.DeviceIdType.MESH,
        )

    def down_copy(step):
        return pltpu.make_async_remote_copy(
            src_ref=down_out.at[step], dst_ref=down_in.at[step],
            send_sem=down_send.at[step], recv_sem=down_recv.at[step],
            device_id=(slab + 1, me), device_id_type=pl.DeviceIdType.MESH,
        )

    def keep(k, value):
        high, low = halves(value)
        products_high[pl.ds(k * probes, probes)] = high
        products_low[pl.ds(k * probes, probes)] = low

    def apply_field(step, value):
        field = value.astype(BF16).reshape(clusters, probes, orb)
        own[step] = field
        fields[step][pl.ds(me * clusters, clusters)] = field

        def send_fields():
            for offset in far + [0]:
                field_copy(step, offset).start()

            @pl.when(slab > 0)
            def _():
                up_copy(step).start()

        def send_down():
            @pl.when(slab < slabs - 1)
            def _():
                down_copy(step).start()

        def send_exchange():
            for offset in far + [0]:
                exchange_copy(step, offset).start()

        if step == 0:
            neighbours = (slab > 0).astype(jnp.int32) + (slab < slabs - 1).astype(jnp.int32)
            pl.semaphore_wait(barrier, chips + neighbours)
        send_fields()
        if step == 0:
            lane = lax.broadcasted_iota(jnp.int32, (1, width), 1)
            group = lane // probes
            inner = lane % probes
            partner_row = jnp.zeros((1, width), jnp.int32)
            source_row = jnp.zeros((1, width), jnp.int32)
            for k in range(pairs):
                partner_row = jnp.where(group == k, partner_ref[k], partner_row)
                source_row = jnp.where(group == k, source_ref[k], source_row)
            device = partner_row // clusters
            partner_row = (
                lax.rem(device, 2) * (half // probes) + device // 2 * clusters + lax.rem(partner_row, clusters)
            )
            partner_row = partner_row * probes + inner
            source_row = source_row * probes + inner
            spread_rows = lax.broadcasted_iota(jnp.int32, spread.shape, 0)
            spread[...] = (spread_rows == partner_row).astype(F32).astype(BF16)
            collect_rows = lax.broadcasted_iota(jnp.int32, collect.shape, 0)
            collect[...] = (collect_rows == source_row).astype(F32).astype(BF16)
        for k in range(pairs):
            if step == 0 and k % part == 0:
                loads[1 + k // part].wait()
            keep(k, plain(own[step, source_ref[k]], blocks[k]))
        high = products_high[...]
        low = products_low[...]
        other = spread[pl.ds((1 - core) * half, half)]
        giving[step] = (plain(other, high) + plain(other, low)).astype(BF16)
        send_exchange()
        if step == 0:
            loads[0].wait()
        for c in range(clusters):
            down_out[step, pl.ds(c * probes, probes)] = plain(field[c], coupling[c]).astype(BF16)
        send_down()
        same = spread[pl.ds(core * half, half)]
        going[step] = plain(same, high) + plain(same, low)

        for offset in far:
            exchange_copy(step, offset).wait_recv()
            mine = going[step, pl.ds(lax.rem(chip + offset, chips) * rows, rows)]
            leaving[step, offset] = (mine + traded[step, offset].astype(F32)).astype(BF16)
            product_copy(step, offset).start()
        for offset in far[::-1]:
            field_copy(step, offset).wait_recv()
            handed_copy(step, offset).start()
        if step == 0:
            loads[1 + CHUNKS].wait()
        local = []
        for c in range(clusters):
            local.append(0.5 * (plain(field[c], onsite[c]) + flipped(field[c], onsite[c])))
        result = jnp.concatenate(local, axis=0)

        field_copy(step, 0).wait_recv()
        exchange_copy(step, 0).wait_recv()
        result = result + going[step, pl.ds(chip * rows, rows)] + traded[step, 0].astype(F32)

        @pl.when(slab < slabs - 1)
        def _():
            up_copy(step).wait_recv()

        @pl.when(slab == slabs - 1)
        def _():
            above[step] = jnp.zeros_like(own[step])

        result = result + jnp.concatenate(
            [flipped(above[step, c], coupling[c]) for c in range(clusters)], axis=0
        )

        @pl.when(slab > 0)
        def _():
            down_copy(step).wait_recv()

        @pl.when(slab == 0)
        def _():
            down_in[step] = jnp.zeros(start.shape, BF16)

        result = result + down_in[step].astype(F32)
        for offset in far:
            handed_copy(step, offset).wait_recv()
        for k in range(pairs):
            keep(k, flipped(fields[step][partner_ref[k]], blocks[k]))
        high = products_high[...]
        low = products_low[...]
        result = result + (plain(collect[...], high) + plain(collect[...], low))
        for offset in far:
            product_copy(step, offset).wait_recv()
            result = result + coming[step, offset].astype(F32)
        return result * factor

    first = apply_field(0, begin)
    first_ref[...] = 0.5 * first.reshape(clusters, probes, orb)
    second = 2.0 * apply_field(1, first) - start[...]
    second_ref[...] = 0.5 * second.reshape(clusters, probes, orb)

    for step in range(2):
        for offset in range(chips):
            field_copy(step, offset).wait_send()
            exchange_copy(step, offset).wait_send()
        for offset in far:
            handed_copy(step, offset).wait_send()
            product_copy(step, offset).wait_send()

        @pl.when(slab > 0)
        def _():
            up_copy(step).wait_send()

        @pl.when(slab < slabs - 1)
        def _():
            down_copy(step).wait_send()


def per_device(phases, onsite, coupling, pair_blocks, pair_source, pair_partner):
    clusters, probes, orb = phases.shape
    pairs = pair_blocks.shape[0]
    slabs = lax.axis_size("slab")
    peers = lax.axis_size("xsec")
    slots = peers * clusters
    rows = clusters * probes
    vmem = pl.BlockSpec(memory_space=pltpu.VMEM)
    smem = pl.BlockSpec(memory_space=pltpu.SMEM)
    hbm = pl.BlockSpec(memory_space=pltpu.HBM)
    dma = pltpu.SemaphoreType.DMA
    out = jax.ShapeDtypeStruct(phases.shape, F32)
    raw = pl.pallas_call(
        functools.partial(kernel, slabs, peers, clusters, pairs, probes, orb),
        out_shape=(out, out),
        in_specs=[smem, smem, hbm, hbm, hbm, hbm],
        out_specs=(vmem, vmem),
        scratch_shapes=[
            pltpu.VMEM((clusters, orb, orb), BF16),
            pltpu.VMEM((clusters, orb, orb), BF16),
            pltpu.VMEM((pairs, orb, orb), BF16),
            pltpu.VMEM((clusters, probes, orb), F32),
            pltpu.VMEM((rows, orb), F32),
            pltpu.VMEM((slots, probes, orb), BF16),
            pltpu.VMEM((slots, probes, orb), BF16),
            pltpu.VMEM((2, clusters, probes, orb), BF16),
            pltpu.VMEM((2, clusters, probes, orb), BF16),
            pltpu.VMEM((2, slots * probes // 2, orb), F32),
            pltpu.VMEM((2, slots * probes // 2, orb), BF16),
            pltpu.VMEM((2, peers // 2, rows, orb), BF16),
            pltpu.VMEM((2, peers // 2, rows, orb), BF16),
            pltpu.VMEM((2, peers // 2, rows, orb), BF16),
            pltpu.VMEM((2, rows, orb), BF16),
            pltpu.VMEM((2, rows, orb), BF16),
            pltpu.VMEM((slots * probes, pairs * probes), BF16),
            pltpu.VMEM((rows, pairs * probes), BF16),
            pltpu.VMEM((pairs * probes, orb), BF16),
            pltpu.VMEM((pairs * probes, orb), BF16),
            dma((3 + CHUNKS,)),
            *[dma((2, peers // 2)) for _ in range(8)],
            dma((2,)), dma((2,)), dma((2,)), dma((2,)),
        ],
        compiler_params=pltpu.CompilerParams(
            collective_id=0, has_side_effects=True, vmem_limit_bytes=63 * 1024 * 1024
        ),
    )(pair_partner, pair_source, phases, onsite, coupling, pair_blocks)
    return 2.0 * raw[0], 2.0 * raw[1]


def solution(mesh):
    spec = P(("slab", "xsec"), None, None)
    flat = P(("slab", "xsec"))
    return jax.shard_map(
        per_device,
        mesh=mesh,
        in_specs=(spec, spec, spec, spec, flat, flat),
        out_specs=(spec, spec),
        check_vma=False,
    )
```
